128 devices in a mesh: blk: 64 (over z, y, x_hi, core), rows: 2 (over x_lo).
Axes of the slice: x: 4 (x_hi: 2, x_lo: 2; x = x_hi * 2 + x_lo), y: 4, z: 4, core: 2. Of those that a mesh axis runs over, the one named last changes fastest.
Arguments:
- panel: bfloat16 [4, 512, 393216], P(None, 'rows', 'blk'), may hold values from -0.009765625 to 0.009765625
- solved: bfloat16 [393216, 1024], P('blk'), may hold values from -6 to 6
- loads: float32 [4, 512, 1024], P(None, 'rows'), may hold values from -6 to 6
- window: bfloat16 [4, 512, 2048], P(None, 'rows'), may hold values from -0.25 to 0.25
- inverses: bfloat16 [4, 512, 512], P(None, 'rows'), as said below
Outputs:
- unknowns: bfloat16 [4, 512, 1024], P(None, 'rows')
The draws below stay inside these ranges and needn't reach their ends.
Inputs may be any that keep to these rules, and one draw needn't show every extreme that they name: inverses[i] is lower triangular, the inverse of the factor's i-th diagonal block.
All inputs are finite; a program needn't handle non-finite values.
Results may differ from the reference program's by a relative error of at most 0.01.
Values may be sent and summed in bfloat16 or wider, within the bound.
A program may use at most 128 MiB of HBM per device.

```python
import math
import jax
import jax.numpy as jnp
from jax import lax

BS = 512
NSTEP = 4
RHS = 1024
PREVC = 393216


def draw_inverses(key, part):
    key_diag, key_lower = jax.random.split(key)
    diagonal = jax.random.uniform(key_diag, (NSTEP, BS), jnp.float32, 0.6, 1.4)
    strict_lower = jax.random.normal(key_lower, (NSTEP, BS, BS), jnp.float32) * (0.8 / math.sqrt(BS))
    row_index = jnp.arange(BS)[:, None]
    col_index = jnp.arange(BS)[None, :]
    below_mask = (col_index < row_index).astype(jnp.float32)
    identity = (col_index == row_index).astype(jnp.float32)
    return (strict_lower * below_mask + diagonal[:, :, None] * identity).astype(jnp.bfloat16)


def level_of(rng, extent, pieces, least, largest):
    factor_of, own = 1.0, jax.random.fold_in(rng, 6)
    for position, blocks in pieces:
        steps = jnp.exp(jax.random.uniform(jax.random.fold_in(own, position), (blocks,), jnp.float32, least / len(pieces), largest / len(pieces)))
        factor_of = factor_of * jnp.repeat(steps, extent[position] // blocks).reshape([-1 if axis == position else 1 for axis in range(len(extent))])
    return factor_of


def gaussian(stream_key, dims, spread, most, cuts=(), dtype=jnp.bfloat16):
    factor_of = level_of(stream_key, dims, cuts, -0.22, 0.18) if cuts else 1.0
    values = jax.random.normal(stream_key, dims, jnp.float32) * spread * factor_of
    return jnp.minimum(jnp.maximum(values, -most), most).astype(dtype)


def setup_inputs(seed: int = 0) -> dict:
    streams_of = jax.random.split(jax.random.key(seed), 6)
    panel = gaussian(streams_of[0], (NSTEP, BS, PREVC), PREVC ** -0.5, 0.009765625, ((1, 2), (2, 64)))
    solved = gaussian(streams_of[1], (PREVC, RHS), 1.0, 6.0, ((0, 64),))
    loads = gaussian(streams_of[2], (NSTEP, BS, RHS), 1.0, 6.0, ((1, 2),), jnp.float32)
    window = gaussian(streams_of[3], (NSTEP, BS, NSTEP * BS), BS ** -0.5, 0.25, ((1, 2),))
    inverses = draw_inverses(jax.random.fold_in(streams_of[5], 71), 0)
    return dict(panel=panel, solved=solved, loads=loads, window=window, inverses=inverses)


def reference(panel, solved, loads, window, inverses):
    def accumulate(index, running):
        offset = (index * BS).astype(jnp.int32)
        columns = lax.dynamic_slice_in_dim(panel, offset, BS, 2).astype(jnp.float32)
        known = lax.dynamic_slice_in_dim(solved, offset, BS, 0).astype(jnp.float32)
        return running + jnp.einsum("ksc,cr->ksr", columns, known, precision=lax.Precision.HIGHEST)

    totals = lax.fori_loop(0, PREVC // BS, accumulate, jnp.zeros((NSTEP, BS, RHS), jnp.float32))
    results = []
    for current in range(NSTEP):
        residual = loads[current] - totals[current]
        for earlier in range(current):
            coupling = window[current][:, earlier * BS:(earlier + 1) * BS]
            residual = residual - jnp.dot(coupling, results[earlier], preferred_element_type=jnp.float32)
        residual = residual.astype(jnp.bfloat16)
        results.append(jnp.dot(inverses[current], residual, preferred_element_type=jnp.float32).astype(jnp.bfloat16))
    return jnp.stack(results)
```

```python
import jax
import jax.numpy as jnp
from jax import lax
from jax.experimental import pallas as pl
from jax.experimental.pallas import tpu as pltpu
from jax.sharding import PartitionSpec as P

F32 = jnp.float32
BF16 = jnp.bfloat16
LANES = 128
KPARTS = 4


def kernel(
    panel_ref, solved_ref, loads_ref, window_ref, inv_ref, out_ref,
    pv, sv, acc, core_out, core_in, a_out, a_in, b_buf, x_buf, loads_v,
    w1, w2, w3, inv_v, u_all, coupled, own_u,
    local_sem, w_send, w_recv, f_send, f_recv, c_send, c_recv,
    a_send, a_recv, b_send, b_recv, x_send, x_recv, g_send, g_recv, p_send, p_recv,
):
    steps, half, depth = pv.shape
    block = 2 * half
    width = sv.shape[2]
    kpart = depth // KPARTS

    blk = lax.axis_index("blk")
    xl = lax.axis_index("rows")
    core = blk % 2
    xh = (blk // 2) % 2
    y = (blk // 4) % 4
    z = blk // 16
    x = xh * 2 + xl
    a = z * (1 - core) + y * core
    b = y * (1 - core) + z * core
    other = 1 - core

    def device(z_, y_, xh_, xl_, core_):
        return {"blk": ((z_ * 4 + y_) * 2 + xh_) * 2 + core_, "rows": xl_}

    partner = device(z, y, xh, xl, other)

    def a_peer(d):
        n = (a + d) % 4
        return device(n * (1 - core) + b * core, b * (1 - core) + n * core, xh, xl, core)

    def b_peer(d):
        n = (b + d) % 4
        return device(a * (1 - core) + n * core, n * (1 - core) + a * core, xh, xl, core)

    def x_peer(d):
        n = (x + d) % 4
        return device(z, y, n // 2, n % 2, core)

    side = [device(z, y, xh, 1 - xl, core), device(z, y, 1 - xh, 1 - xl, core)]

    def remote(src, dst, send, recv, target):
        return pltpu.make_async_remote_copy(
            src_ref=src, dst_ref=dst, send_sem=send, recv_sem=recv,
            device_id=target, device_id_type=pl.DeviceIdType.MESH,
        )

    started = []

    def go(copy):
        copy.start()
        started.append(copy)

    def cols(core_, a_):
        return pl.ds(pl.multiple_of(core_ * width + a_ * LANES, LANES), LANES)

    head = []
    for k in range(KPARTS):
        ks = pl.ds(k * kpart, kpart)
        head.append((
            pltpu.make_async_copy(panel_ref.at[0, :, ks], pv.at[0, :, ks], local_sem.at[2 * k]),
            pltpu.make_async_copy(
                solved_ref.at[ks, pl.ds(pl.multiple_of(other * width, width), width)],
                sv.at[0, ks, :], local_sem.at[2 * k + 1]),
        ))
    base = 2 * KPARTS
    own_half = pltpu.make_async_copy(
        solved_ref.at[:, pl.ds(pl.multiple_of(core * width, width), width)],
        sv.at[1], local_sem.at[base])
    panels = [None] + [
        pltpu.make_async_copy(panel_ref.at[i], pv.at[i], local_sem.at[base + i])
        for i in range(1, steps)
    ]
    windows = [None, w1, w2, w3]
    small = [
        pltpu.make_async_copy(loads_ref.at[:, :, cols(core, a)], loads_v, local_sem.at[base + 4]),
        pltpu.make_async_copy(inv_ref, inv_v.at[:, xl], local_sem.at[base + 5]),
    ] + [
        pltpu.make_async_copy(
            window_ref.at[i, :, pl.ds(0, i * block)], windows[i].at[xl], local_sem.at[base + 5 + i])
        for i in range(1, steps)
    ]

    for pair in head[:3]:
        for copy in pair:
            copy.start()

    barrier = pltpu.get_barrier_semaphore()
    greeted = [partner]
    for d in (1, 2, 3):
        greeted += [a_peer(d), b_peer(d), x_peer(d)]
    for peer in greeted:
        pl.semaphore_signal(barrier, inc=1, device_id=peer, device_id_type=pl.DeviceIdType.MESH)

    quarter = half // 4

    def share(d, core_):
        return pl.ds(pl.multiple_of((d * 2 + core_) * quarter, quarter), quarter)

    def factor_views(rows_half, rows):
        return [inv_v.at[pl.ds(0, steps - 1), rows_half, rows, :]] + [
            windows[i].at[rows_half, rows, :] for i in range(1, steps)
        ]

    def factor_send(d):
        rows = share(d, core)
        sources = [inv_ref.at[pl.ds(0, steps - 1), rows, :]] + [
            window_ref.at[i, rows, pl.ds(0, i * block)] for i in range(1, steps)
        ]
        return [
            remote(s, t, w_send.at[d, j], w_recv.at[d, j], side[d])
            for j, (s, t) in enumerate(zip(sources, factor_views(xl, rows)))
        ]

    def factor_arrive(d):
        views = factor_views(1 - xl, share(d, core))
        return [remote(v, v, w_send.at[d, j], w_recv.at[d, j], side[d]) for j, v in enumerate(views)]

    def factor_forward(d):
        views = factor_views(1 - xl, share(d, core))
        return [remote(v, v, f_send.at[d, j], f_recv.at[d, j], partner) for j, v in enumerate(views)]

    def factor_forwarded(d):
        views = factor_views(1 - xl, share(d, other))
        return [remote(v, v, f_send.at[d, j], f_recv.at[d, j], partner) for j, v in enumerate(views)]

    def forward_factor(parts):
        for j in parts:
            for d in (0, 1):
                factor_arrive(d)[j].wait_recv()
                go(factor_forward(d)[j])

    def core_copy(i):
        return remote(core_out.at[i], core_in.at[i], c_send.at[i], c_recv.at[i], partner)

    def send_core(i):
        core_out[i] = acc[...].astype(BF16)
        go(core_copy(i))

    def a_copy(i, d):
        return remote(a_out.at[i, (a + d) % 4], a_in.at[i, d - 1],
                      a_send.at[i, d - 1], a_recv.at[i, d - 1], a_peer(d))

    def send_a(i):
        core_copy(i).wait_recv()
        for n in range(4):
            at = slice(n * LANES, (n + 1) * LANES)
            a_out[i, n] = (acc[:, at] + core_in[i, :, at].astype(F32)).astype(BF16)
        for d in (2, 1, 3):
            go(a_copy(i, d))

    def b_copy(i, d):
        return remote(b_buf.at[i, b], b_buf.at[i, b], b_send.at[i, d - 1], b_recv.at[i, d - 1], b_peer(d))

    def send_b(i):
        total = a_out[i, a].astype(F32)
        for d in (1, 3, 2):
            a_copy(i, d).wait_recv()
            total = total + a_in[i, d - 1].astype(F32)
        b_buf[i, b] = total.astype(BF16)
        for d in (2, 1, 3):
            go(b_copy(i, d))

    def x_copy(i, d):
        return remote(x_buf.at[i, x], x_buf.at[i, x], x_send.at[i, d - 1], x_recv.at[i, d - 1], x_peer(d))

    def send_x(i):
        for d in (1, 3, 2):
            b_copy(i, d).wait_recv()
        total = (b_buf[i, 0].astype(F32) + b_buf[i, 1].astype(F32)) + (
            b_buf[i, 2].astype(F32) + b_buf[i, 3].astype(F32))
        total = loads_v[i] * (1 - xh).astype(F32) - total
        x_buf[i, x] = total.astype(BF16)
        for d in (2, 1, 3):
            go(x_copy(i, d))

    def g_copy(i, d):
        mine = out_ref.at[i, :, cols(core, a)]
        return remote(own_u.at[i], mine, g_send.at[i, d - 1], g_recv.at[i, d - 1], a_peer(d))

    def p_copy(i, d):
        view = out_ref.at[i, :, cols(core, (a - d + 4) % 4)]
        source = own_u.at[i] if d == 0 else view
        return remote(source, view, p_send.at[i, d], p_recv.at[i, d], partner)

    def p_arrive(i, d):
        view = out_ref.at[i, :, cols(other, (b - d + 4) % 4)]
        return remote(view, view, p_send.at[i, d], p_recv.at[i, d], partner)

    def solve(i):
        for d in (1, 3, 2):
            x_copy(i, d).wait_recv()
        upper = x_buf[i, 0].astype(F32) + x_buf[i, 2].astype(F32)
        lower = x_buf[i, 1].astype(F32) + x_buf[i, 3].astype(F32)
        residual = jnp.concatenate([upper, lower], axis=0)
        if i > 0:
            residual = residual - coupled[...]
        residual = residual.astype(BF16)
        if i < steps - 1:
            u_all[pl.ds(i * block, block), :] = jnp.dot(
                inv_v[i].reshape(block, block), residual, preferred_element_type=F32).astype(BF16)
            mine = u_all[pl.ds(pl.multiple_of(i * block + xl * half, half), half), :]
        else:
            mine = jnp.dot(inv_v[i, xl], residual, preferred_element_type=F32).astype(BF16)
        own_u[i] = mine
        out_ref[i, :, cols(core, a)] = mine
        for d in (2, 1, 3):
            go(g_copy(i, d))
        go(p_copy(i, 0))
        if i < steps - 1:
            known = (i + 1) * block
            coupled[...] = jnp.dot(
                windows[i + 1][...].reshape(block, known), u_all[pl.ds(0, known), :],
                preferred_element_type=F32)

    def forward(i):
        for d in (1, 3, 2):
            view = out_ref.at[i, :, cols(core, (a - d + 4) % 4)]
            remote(own_u.at[i], view, g_send.at[i, d - 1], g_recv.at[i, d - 1], a_peer(d)).wait_recv()
            go(p_copy(i, d))

    for k in range(KPARTS):
        for copy in head[k]:
            copy.wait()
        if k + 3 < KPARTS:
            for copy in head[k + 3]:
                copy.start()
        elif k + 3 == KPARTS:
            own_half.start()
        elif k + 2 == KPARTS:
            panels[1].start()
        ks = pl.ds(k * kpart, kpart)
        part = jnp.dot(pv[0, :, ks], sv[0, ks, :], preferred_element_type=F32)
        acc[...] = part if k == 0 else acc[...] + part
        if k == 1:
            pl.semaphore_wait(barrier, len(greeted))
            for d in (0, 1):
                for copy in factor_send(d):
                    go(copy)
    send_core(0)
    for copy in panels[2:] + small:
        copy.start()

    def multiply(i, h):
        acc[...] = jnp.dot(pv[i], sv[h], preferred_element_type=F32)

    own_half.wait()
    multiply(0, 1)
    send_a(0)

    panels[1].wait()
    multiply(1, 0)
    send_core(1)
    multiply(1, 1)
    send_a(1)
    send_b(0)

    panels[2].wait()
    multiply(2, 0)
    send_core(2)
    multiply(2, 1)
    send_a(2)
    send_b(1)
    for copy in small:
        copy.wait()
    send_x(0)

    panels[3].wait()
    multiply(3, 0)
    send_core(3)
    forward_factor((0, 1))
    multiply(3, 1)
    send_a(3)
    send_b(2)
    forward_factor((2, 3))
    send_x(1)

    for d in (0, 1):
        for copy in factor_forwarded(d):
            copy.wait_recv()
    solve(0)
    send_b(3)
    send_x(2)
    solve(1)
    forward(0)
    send_x(3)
    solve(2)
    forward(1)
    solve(3)
    forward(2)
    forward(3)
    for i in range(steps):
        for d in range(4):
            p_arrive(i, d).wait_recv()
    for copy in started:
        copy.wait_send()


def shards(panel, solved, loads, window, inverses):
    steps, half, depth = panel.shape
    rhs = solved.shape[1]
    block = 2 * half
    width = rhs // 2
    vm = pltpu.VMEM
    dma = pltpu.SemaphoreType.DMA
    piece = (half, LANES)
    return pl.pallas_call(
        kernel,
        out_shape=pltpu.VMEM((steps, half, rhs), BF16),
        in_specs=[pl.BlockSpec(memory_space=pl.ANY)] * 5,
        out_specs=pl.BlockSpec(memory_space=pltpu.VMEM),
        scratch_shapes=[
            vm((steps, half, depth), BF16),
            vm((2, depth, width), BF16),
            vm((half, width), F32),
            vm((steps, half, width), BF16),
            vm((steps, half, width), BF16),
            vm((steps, 4) + piece, BF16),
            vm((steps, 3) + piece, BF16),
            vm((steps, 4) + piece, BF16),
            vm((steps, 4) + piece, BF16),
            vm((steps,) + piece, F32),
            vm((2, half, block), BF16),
            vm((2, half, 2 * block), BF16),
            vm((2, half, 3 * block), BF16),
            vm((steps, 2, half, block), BF16),
            vm(((steps - 1) * block, LANES), BF16),
            vm((block, LANES), F32),
            vm((steps,) + piece, BF16),
            dma((2 * KPARTS + 9,)),
            dma((2, 4)), dma((2, 4)), dma((2, 4)), dma((2, 4)),
            dma((steps,)), dma((steps,)),
            dma((steps, 3)), dma((steps, 3)),
            dma((steps, 3)), dma((steps, 3)),
            dma((steps, 3)), dma((steps, 3)),
            dma((steps, 3)), dma((steps, 3)),
            dma((steps, 4)), dma((steps, 4)),
        ],
        compiler_params=pltpu.CompilerParams(
            collective_id=0, has_side_effects=True, vmem_limit_bytes=56 * 2**20),
    )(panel, solved, loads, window, inverses)


def solution(mesh):
    placed = (
        P(None, "rows", "blk"),
        P("blk", None),
        P(None, "rows", None),
        P(None, "rows", None),
        P(None, "rows", None),
    )
    return jax.shard_map(
        shards, mesh=mesh, in_specs=placed, out_specs=P(None, "rows", None), check_vma=False
    )
```
